32 devices in a mesh: group: 4 (over x, core), dev: 8 (over z, y).
Axes of the slice: x: 2, y: 2, z: 4, core: 2. Of those that a mesh axis runs over, the one named last changes fastest.
Arguments:
- features: bfloat16 [131072, 128], P(('group', 'dev')), may hold values from -6 to 6
- coords: bfloat16 [3, 131072], P(None, ('group', 'dev')), may hold values from 0 to 1
- near_pairs: int32 [2, 256], P(None, 'group'), may hold values from 0 to 127, as said below
- parent_two: int32 [512], P(('group', 'dev')), may hold values from 0 to 31, as said below
- parent_three: int32 [128], P('group'), may hold values from 0 to 7
- rates: float32 [4], replicated, may hold values from 6 to 40
- w_near: bfloat16 [128, 128], replicated, may hold values from -0.5 to 0.5
- restrict: bfloat16 [64, 256], replicated, may hold values from -0.375 to 0.375
- w_two: bfloat16 [128, 128], replicated, may hold values from -0.5 to 0.5
- w_three: bfloat16 [128, 128], replicated, may hold values from -0.5 to 0.5
- w_four: bfloat16 [128, 128], replicated, may hold values from -0.5 to 0.5
- coupling: bfloat16 [32, 32], replicated, may hold values from -1 to 1
- expand: bfloat16 [256, 64], replicated, may hold values from -0.75 to 0.75
- w_out: bfloat16 [128, 128], replicated, may hold values from -0.5 to 0.5
Outputs:
- mixed: bfloat16 [131072, 128], P(('group', 'dev'))
The draws below stay inside these ranges and needn't reach their ends.
Inputs may be any that keep to these rules, and one draw needn't show every extreme that they name: `near_pairs`: for any two devices A and P of dev in one region, at most 2 near pairs of that region have their first block on A and their second on P, and in each region some such two devices have exactly 2. `parent_two`: every level-two node of a region is named by exactly four blocks of that region.
All inputs are finite; a program needn't handle non-finite values.
Results may differ from the reference program's by a relative error of at most 0.008.
Values may be sent and summed in bfloat16 or wider, within the bound.
A program may use at most 128 MiB of HBM per device.

```python
import math
import jax
import jax.numpy as jnp
from jax import lax

C = 128
H = 4
B = 256
S = 64
BLK_DEV = 16
CAP = 2
NODES3_GROUP = 8
BLOCKS = 512
POINTS = 131072
BLK_GROUP = 128
PAIRS_GROUP = 64
PAIRS = 256
NODES2_GROUP = 32
NODES2 = 128
NODES3 = 32


def draw_near_pairs(key, part):
    groups_n = PAIRS // PAIRS_GROUP
    devices_n = BLK_GROUP // BLK_DEV
    slots_all = devices_n * devices_n * CAP

    def one_group(group_key):
        keys = jax.random.split(group_key, 5)
        shuffled = jax.random.permutation(keys[0], slots_all).astype(jnp.int32)
        offsets = jax.random.randint(keys[1], (devices_n,), 0, slots_all).astype(jnp.int32)
        slot_ids = jnp.arange(slots_all, dtype=jnp.int32)
        owner_first = slot_ids // (devices_n * CAP)
        owner_second = slot_ids // CAP % devices_n
        score = (shuffled + offsets[owner_first]) * slots_all + slot_ids
        forced = jax.random.randint(keys[2], (), 0, devices_n * devices_n).astype(jnp.int32)
        score = jnp.where(slot_ids // CAP == forced, -1 - slot_ids % CAP, score)
        picked = jnp.argsort(score, stable=True)[:PAIRS_GROUP]
        first_local = jax.random.randint(keys[3], (PAIRS_GROUP,), 0, BLK_DEV).astype(jnp.int32)
        second_local = jax.random.randint(keys[4], (PAIRS_GROUP,), 0, BLK_DEV).astype(jnp.int32)
        first_block = owner_first[picked] * BLK_DEV + first_local
        second_block = owner_second[picked] * BLK_DEV + second_local
        return jnp.stack([first_block, second_block])
    stacked = jax.vmap(one_group)(jax.random.split(jax.random.fold_in(key, 17), groups_n))
    return stacked.transpose(1, 0, 2).reshape(2, PAIRS).astype(jnp.int32)


def draw_parent_two(key, part):
    groups_n = BLOCKS // BLK_GROUP

    def one_group(group_key):
        order = jax.random.permutation(group_key, BLK_GROUP).astype(jnp.int32)
        return order // 4
    stacked = jax.vmap(one_group)(jax.random.split(jax.random.fold_in(key, 23), groups_n))
    return stacked.reshape(BLOCKS).astype(jnp.int32)


def place_ends(array, key, low, high):
    place = [jax.random.randint(jax.random.fold_in(key, axis), (), 0, length) for axis, length in enumerate(array.shape)]
    longest = array.shape.index(max(array.shape))
    next_to = place[:longest] + [(place[longest] + 1) % array.shape[longest]] + place[longest + 1:]
    return array.at[tuple(place)].set(low).at[tuple(next_to)].set(high)


def shard_levels(stream_key, dims, pieces, least, top_value):
    level, own = 1.0, jax.random.fold_in(stream_key, 6)
    for axis_at, parts in pieces:
        heights = jnp.exp(jax.random.uniform(jax.random.fold_in(own, axis_at), (parts,), jnp.float32, least / len(pieces), top_value / len(pieces)))
        level = level * jnp.repeat(heights, dims[axis_at] // parts).reshape([-1 if axis == axis_at else 1 for axis in range(len(dims))])
    return level


def gaussian(key, extent, width, limit, pieces=(), held_as=jnp.bfloat16):
    entries = jax.random.normal(key, extent, jnp.float32) * width
    if len(pieces) > 0:
        entries = shard_levels(key, extent, pieces, -0.22, 0.18) * entries
    return jnp.clip(entries, min=-limit, max=limit).astype(held_as)


def setup_inputs(seed: int = 0) -> dict:
    key_list = jax.random.split(jax.random.key(seed), 15)
    features = gaussian(key_list[0], (POINTS, C), 1.0, 6.0, ((0, 32),))
    coords = jnp.clip(1.0 * jax.random.uniform(key_list[1], (3, POINTS), jnp.float32) ** shard_levels(key_list[1], (3, POINTS), ((1, 32),), -0.2, 0.2), 0.0, 1.0).astype(jnp.bfloat16)
    near_pairs = draw_near_pairs(jax.random.fold_in(key_list[14], 71), 0)
    parent_two = draw_parent_two(jax.random.fold_in(key_list[14], 71), 0)
    parent_three = place_ends(jax.random.randint(key_list[4], (NODES2,), 0, NODES3_GROUP), jax.random.fold_in(key_list[4], 1), 0, NODES3_GROUP - 1).astype(jnp.int32)
    rates = jnp.clip(jnp.exp(jax.random.uniform(key_list[5], (H,), jnp.float32, math.log(6.0), math.log(40.0))), 6.0, 40.0)
    w_near = gaussian(key_list[6], (C, C), C ** -0.5, 0.5)
    restrict = gaussian(key_list[7], (S, B), B ** -0.5, 0.375)
    w_two = gaussian(key_list[8], (C, C), C ** -0.5, 0.5)
    w_three = gaussian(key_list[9], (C, C), C ** -0.5, 0.5)
    w_four = gaussian(key_list[10], (C, C), C ** -0.5, 0.5)
    coupling = gaussian(key_list[11], (NODES3, NODES3), NODES3 ** -0.5, 1.0)
    expand = gaussian(key_list[12], (B, S), S ** -0.5, 0.75)
    w_out = gaussian(key_list[13], (C, C), C ** -0.5, 0.5)
    return dict(features=features, coords=coords, near_pairs=near_pairs, parent_two=parent_two, parent_three=parent_three, rates=rates, w_near=w_near, restrict=restrict, w_two=w_two, w_three=w_three, w_four=w_four, coupling=coupling, expand=expand, w_out=w_out)


def kernel_table(cloud_one, cloud_two, rates):
    first_pos = cloud_one.astype(jnp.float32)
    second_pos = cloud_two.astype(jnp.float32)
    delta_x = first_pos[:, 0, :, None] - second_pos[:, 0, None, :]
    delta_y = first_pos[:, 1, :, None] - second_pos[:, 1, None, :]
    delta_z = first_pos[:, 2, :, None] - second_pos[:, 2, None, :]
    distance = delta_x * delta_x + delta_y * delta_y + delta_z * delta_z
    return jnp.exp(-rates[None, :, None, None] * distance[:, None]).astype(jnp.bfloat16)


def apply_table(kernel, block_values, head_count, transposed):
    blocks_n, points_n, channels = block_values.shape
    by_head = block_values.reshape(blocks_n, points_n, head_count, channels // head_count)
    form = "nhqp,nqhc->nphc" if transposed else "nhpq,nqhc->nphc"
    result = jnp.einsum(form, kernel.astype(jnp.float32), by_head.astype(jnp.float32))
    return result.reshape(blocks_n, points_n, channels)


def reference(features, coords, near_pairs, parent_two, parent_three, rates, w_near, restrict, w_two, w_three, w_four, coupling, expand, w_out):
    head_count = rates.shape[0]
    values = jnp.dot(features, w_near, preferred_element_type=jnp.float32).astype(jnp.bfloat16)
    vblocks = values.reshape(BLOCKS, B, C)
    cblocks = coords.reshape(3, BLOCKS, B).transpose(1, 0, 2)

    def self_term(operands):
        cloud, block_values = operands
        return apply_table(kernel_table(cloud, cloud, rates), block_values, head_count, False)

    near_field = lax.map(self_term, (cblocks.reshape(-1, 8, 3, B), vblocks.reshape(-1, 8, B, C))).reshape(BLOCKS, B, C)
    pair_group = jnp.arange(PAIRS, dtype=jnp.int32) // PAIRS_GROUP
    first_ids = near_pairs[0] + pair_group * BLK_GROUP
    second_ids = near_pairs[1] + pair_group * BLK_GROUP

    def pair_step(running, batch_pairs):
        first_batch, second_batch = batch_pairs
        kernel = kernel_table(cblocks[first_batch], cblocks[second_batch], rates)
        side_first = apply_table(kernel, vblocks[second_batch], head_count, False)
        side_second = apply_table(kernel, vblocks[first_batch], head_count, True)
        side_second = lax.optimization_barrier(side_second.astype(jnp.bfloat16)).astype(jnp.float32)
        running = running.at[first_batch].add(side_first)
        running = running.at[second_batch].add(side_second)
        return running, None

    near_field, _ = lax.scan(pair_step, near_field, (first_ids.reshape(-1, 32), second_ids.reshape(-1, 32)))

    level_one = jnp.einsum("sb,nbc->nsc", restrict.astype(jnp.float32), features.reshape(BLOCKS, B, C).astype(jnp.float32)).astype(jnp.bfloat16)
    block_group = jnp.arange(BLOCKS, dtype=jnp.int32) // BLK_GROUP
    node_two = block_group * NODES2_GROUP + parent_two
    level_two_sum = jax.ops.segment_sum(level_one.astype(jnp.float32), node_two, NODES2).astype(jnp.bfloat16)
    level_two = jax.nn.gelu(jnp.dot(level_two_sum.reshape(-1, C), w_two, preferred_element_type=jnp.float32)).astype(jnp.bfloat16).reshape(NODES2, S, C)
    node_group = jnp.arange(NODES2, dtype=jnp.int32) // NODES2_GROUP
    node_three = node_group * NODES3_GROUP + parent_three
    level_three = (jax.ops.segment_sum(level_two.astype(jnp.float32), node_three, NODES3) * (NODES3_GROUP / NODES2_GROUP)).astype(jnp.bfloat16)
    mixed_three = jnp.dot(coupling, level_three.reshape(NODES3, S * C), preferred_element_type=jnp.float32).astype(jnp.bfloat16)
    down_three = jax.nn.gelu(jnp.dot(mixed_three.reshape(-1, C), w_three, preferred_element_type=jnp.float32)).astype(jnp.bfloat16).reshape(NODES3, S, C)
    lifted = jnp.dot(level_two.reshape(-1, C), w_four, preferred_element_type=jnp.float32).reshape(NODES2, S, C)
    down_two = jax.nn.gelu(lifted + down_three[node_three].astype(jnp.float32)).astype(jnp.bfloat16)
    far_field = jnp.einsum("bs,nsc->nbc", expand.astype(jnp.float32), down_two[node_two].astype(jnp.float32)).astype(jnp.bfloat16)
    total = near_field.reshape(POINTS, C) * (B ** -0.5) + jnp.dot(far_field.reshape(POINTS, C), w_out, preferred_element_type=jnp.float32)
    return total.astype(jnp.bfloat16)
```

```python
import functools
import math

import jax
import jax.numpy as jnp
from jax import lax
from jax.experimental import pallas as pl
from jax.experimental.pallas import tpu as pltpu
from jax.sharding import PartitionSpec as P

CAP = 2
SLOTS = 2 * CAP
AUG = 16
ROWS = 8
LOG2E = math.log2(math.e)
MESH = pl.DeviceIdType.MESH
F32 = jnp.float32
BF16 = jnp.bfloat16


def mm(a, b):
    return jnp.dot(a, b, preferred_element_type=F32)


def iota(shape, axis):
    return lax.broadcasted_iota(jnp.int32, shape, axis)


def prepare(
    n_dev,
    pairs_ref,
    feat_ref,
    coords_ref,
    par_ref,
    wnear_ref,
    restrict_ref,
    vals_ref,
    pos_p_ref,
    pos_q_ref,
    send_v_ref,
    send_q_ref,
    pick_p_ref,
    partial_ref,
    index_ref,
    count_ref,
    level_ref,
):
    me = lax.axis_index("dev")
    blocks, points, channels = vals_ref.shape
    pairs_n = pairs_ref.shape[1]
    s_rows, nodes, _ = partial_ref.shape

    def clear(i, _):
        index_ref[i] = -1
        return 0

    lax.fori_loop(0, n_dev * SLOTS, clear, 0)

    def clear_count(i, _):
        count_ref[i] = 0
        return 0

    lax.fori_loop(0, n_dev * 2, clear_count, 0)

    def one_pair(k, _):
        a = pairs_ref[0, k]
        b = pairs_ref[1, k]
        own_a = a // blocks
        own_b = b // blocks

        @pl.when(own_a == me)
        def _():
            rank = count_ref[own_b]
            index_ref[own_b * SLOTS + rank] = a % blocks
            count_ref[own_b] = rank + 1

        @pl.when(own_b == me)
        def _():
            rank = count_ref[n_dev + own_a]
            index_ref[own_a * SLOTS + CAP + rank] = b % blocks
            count_ref[n_dev + own_a] = rank + 1

        return 0

    lax.fori_loop(0, pairs_n, one_pair, 0)

    xyz = coords_ref[...].astype(F32)
    norm = jnp.sum(xyz * xyz, axis=0, keepdims=True)
    one = norm.astype(BF16).astype(F32)
    two = (norm - one).astype(BF16).astype(F32)
    three = norm - one - two
    ones = jnp.ones_like(norm)
    pad = jnp.zeros((AUG - 9, norm.shape[1]), F32)
    aug_p = jnp.concatenate([-2.0 * xyz, one, two, three, ones, ones, ones, pad], axis=0).astype(BF16)
    aug_q = jnp.concatenate([xyz, ones, ones, ones, one, two, three, pad], axis=0).astype(BF16)
    for j in range(blocks):
        pos_p_ref[j] = aug_p[:, j * points : (j + 1) * points]
        pos_q_ref[j] = aug_q[:, j * points : (j + 1) * points]
        block = feat_ref[pl.ds(j * points, points), :]
        vals_ref[j] = mm(block, wnear_ref[...]).astype(BF16)
        level_ref[j] = mm(restrict_ref[...], block).astype(BF16).astype(F32)

    rows, cols = ROWS * nodes, blocks * ROWS
    row, col = iota((rows, cols), 0), iota((rows, cols), 1)
    spread = ((row // nodes == col % ROWS) & (row % nodes == par_ref[...])).astype(F32).astype(BF16)
    for c in range(s_rows // ROWS):
        part = level_ref[:, c * ROWS : (c + 1) * ROWS, :].reshape(cols, channels).astype(BF16)
        partial_ref[c * ROWS : (c + 1) * ROWS] = (
            mm(spread, part).astype(BF16).reshape(ROWS, nodes, channels)
        )

    def pick(i, _):
        local = jnp.maximum(index_ref[i], 0)
        to = (i // SLOTS) * SLOTS + (i + CAP) % SLOTS
        send_v_ref[to] = vals_ref[local]
        send_q_ref[to] = pos_q_ref[local]
        pick_p_ref[i] = pos_p_ref[local]
        return 0

    lax.fori_loop(0, n_dev * SLOTS, pick, 0)


def table_apply(pos_p, pos_q, values, rates_ref, heads):
    d2 = lax.dot_general(pos_p, pos_q, (((0,), (0,)), ((), ())), preferred_element_type=F32)
    channels = values.shape[1]
    head_of = iota(values.shape, 1) // (channels // heads)
    total = None
    for h in range(heads):
        kernel = jnp.exp2((d2 * (rates_ref[h] * (-LOG2E))).astype(BF16))
        term = mm(kernel, jnp.where(head_of == h, values, jnp.zeros_like(values)))
        total = term if total is None else total + term
    return total


def exchange(
    n_dev,
    n_group,
    rates_ref,
    vals_ref,
    pos_p_ref,
    pos_q_ref,
    pick_p_ref,
    send_v_ref,
    send_q_ref,
    partial_ref,
    p3_lane_ref,
    p3_col_ref,
    wtwo_ref,
    wthree_ref,
    wfour_ref,
    coupling_ref,
    self_ref,
    side_ref,
    down_ref,
    got_v,
    got_q,
    got_part,
    got_three,
    got_down,
    three_buf,
    down_buf,
    v_sems,
    q_sems,
    part_sems,
    three_sems,
    down_sems,
    local_sems,
):
    me = lax.axis_index("dev")
    mine = lax.axis_index("group")
    heads = rates_ref.shape[0]
    blocks = vals_ref.shape[0]
    channels = vals_ref.shape[2]
    slice_rows, nodes, _ = got_part.shape[1:]
    nodes3 = coupling_ref.shape[0] // n_group

    def ahead(k):
        return (me + k) % n_dev

    barrier = pltpu.get_barrier_semaphore()

    def greet(k, _):
        pl.semaphore_signal(barrier, inc=1, device_id={"dev": ahead(k)}, device_id_type=MESH)
        return 0

    def greet_group(k, _):
        pl.semaphore_signal(barrier, inc=1, device_id={"group": (mine + k) % n_group}, device_id_type=MESH)
        return 0

    lax.fori_loop(1, n_dev, greet, 0)
    lax.fori_loop(1, n_group, greet_group, 0)

    def own_copies():
        return (
            pltpu.make_async_copy(partial_ref.at[pl.ds(me * slice_rows, slice_rows)], got_part.at[me], local_sems.at[0]),
            pltpu.make_async_copy(send_v_ref.at[me], got_v.at[me], local_sems.at[1]),
            pltpu.make_async_copy(send_q_ref.at[me], got_q.at[me], local_sems.at[2]),
        )

    for copy in own_copies():
        copy.start()
    pl.semaphore_wait(barrier, n_dev - 1 + n_group - 1)

    def dev_copy(src, dst, sems, k):
        return pltpu.make_async_remote_copy(
            src_ref=src,
            dst_ref=dst,
            send_sem=sems.at[0, k],
            recv_sem=sems.at[1, k],
            device_id={"dev": ahead(k)},
            device_id_type=MESH,
        )

    def part_copy(k):
        return dev_copy(
            partial_ref.at[pl.ds(ahead(k) * slice_rows, slice_rows)], got_part.at[me], part_sems, k
        )

    def v_copy(k):
        return dev_copy(send_v_ref.at[ahead(k)], got_v.at[me], v_sems, k)

    def q_copy(k):
        return dev_copy(send_q_ref.at[ahead(k)], got_q.at[me], q_sems, k)

    def down_copy(k):
        return dev_copy(down_buf, got_down.at[me], down_sems, k)

    def three_copy(k):
        return pltpu.make_async_remote_copy(
            src_ref=three_buf,
            dst_ref=got_three.at[mine],
            send_sem=three_sems.at[0, k],
            recv_sem=three_sems.at[1, k],
            device_id={"group": (mine + k) % n_group},
            device_id_type=MESH,
        )

    def each(fn, count):
        def body(k, _):
            fn(k)
            return 0

        lax.fori_loop(1, count, body, 0)

    each(lambda k: part_copy(k).start(), n_dev)
    each(lambda k: (q_copy(k).start(), v_copy(k).start()), n_dev)

    def self_tables(low, high):
        def body(j, _):
            self_ref[j] = table_apply(pos_p_ref[j], pos_q_ref[j], vals_ref[j], rates_ref, heads)
            return 0

        lax.fori_loop(low, high, body, 0)

    quarter = blocks // 4
    self_tables(0, quarter)
    for copy in own_copies():
        copy.wait()
    each(lambda k: part_copy(k).wait(), n_dev)

    rows = slice_rows * nodes
    rows3 = slice_rows * nodes3
    total = got_part[0].astype(F32)
    for d in range(1, n_dev):
        total = total + got_part[d].astype(F32)
    flat = total.reshape(rows, channels).astype(BF16)
    two = jax.nn.gelu(mm(flat, wtwo_ref[...])).astype(BF16)
    row, col = iota((rows3, rows), 0), iota((rows3, rows), 1)
    select = ((row // nodes3 == col // nodes) & (row % nodes3 == p3_lane_ref[...])).astype(F32).astype(BF16)
    three_buf[...] = (mm(select, two) * (nodes3 / nodes)).astype(BF16)
    lifted = mm(two, wfour_ref[...])
    self_tables(quarter, quarter + 1)
    each(lambda k: three_copy(k).start(), n_group)
    got_three[mine] = three_buf[...]
    self_tables(quarter + 1, 2 * quarter + quarter // 2)

    all3 = coupling_ref.shape[0]
    row, col = iota((rows3, all3), 0), iota((rows3, all3), 1)
    left = mm((col == mine * nodes3 + row % nodes3).astype(F32).astype(BF16), coupling_ref[...]).astype(BF16)
    row, col = iota((all3, n_group * rows3), 0), iota((all3, n_group * rows3), 1)
    right = (row == (col // rows3) * nodes3 + col % nodes3).astype(F32).astype(BF16)
    row, col = iota((rows3, n_group * rows3), 0), iota((rows3, n_group * rows3), 1)
    wide = jnp.where(row // nodes3 == (col % rows3) // nodes3, mm(left, right), 0.0).astype(BF16)
    row, col = iota((rows, rows3), 0), iota((rows, rows3), 1)
    lift = ((row // nodes == col // nodes3) & (p3_col_ref[...] == col % nodes3)).astype(F32).astype(BF16)

    each(lambda k: three_copy(k).wait(), n_group)
    mixed = mm(wide, got_three[...].reshape(n_group * rows3, channels)).astype(BF16)
    down3 = jax.nn.gelu(mm(mixed, wthree_ref[...])).astype(BF16)
    down2 = jax.nn.gelu(lifted + mm(lift, down3)).astype(BF16).reshape(slice_rows, nodes, channels)
    down_buf[...] = down2
    got_down[me] = down2
    self_tables(2 * quarter + quarter // 2, 2 * quarter + quarter // 2 + 1)
    each(lambda k: down_copy(k).start(), n_dev)
    self_tables(2 * quarter + quarter // 2 + 1, blocks)

    def side_of(k, _):
        source = (me + n_dev - k) % n_dev

        @pl.when(k > 0)
        def _():
            q_copy(k).wait()
            v_copy(k).wait()

        def one(j, _):
            side_ref[source, j] = table_apply(
                pick_p_ref[source, j], got_q[source, j], got_v[source, j], rates_ref, heads
            ).astype(BF16)
            return 0

        lax.fori_loop(0, SLOTS, one, 0)
        return 0

    lax.fori_loop(0, n_dev, side_of, 0)
    each(lambda k: down_copy(k).wait(), n_dev)
    down_ref[...] = got_down[...]


def finish(slots_n, index_ref, self_ref, side_ref, down_ref, par_ref, expand_ref, wout_ref, out_ref, acc, parent_down):
    blocks, points, channels = self_ref.shape
    s_rows, nodes, _ = down_ref.shape
    rows, cols = blocks * ROWS, ROWS * nodes
    row, col = iota((rows, cols), 0), iota((rows, cols), 1)
    gather = ((row % ROWS == col // nodes) & (par_ref[...] == col % nodes)).astype(F32).astype(BF16)
    for c in range(s_rows // ROWS):
        part = down_ref[c * ROWS : (c + 1) * ROWS].reshape(cols, channels)
        parent_down[:, c * ROWS : (c + 1) * ROWS, :] = mm(gather, part).reshape(blocks, ROWS, channels)
    acc[...] = self_ref[...]

    def add(i, _):
        local = index_ref[i]

        @pl.when(local >= 0)
        def _():
            acc[local] += side_ref[i].astype(F32)

        return 0

    lax.fori_loop(0, slots_n, add, 0)
    for j in range(blocks):
        far = mm(expand_ref[...], parent_down[j].astype(BF16)).astype(BF16)
        total = acc[j] * (points ** (-0.5)) + mm(far, wout_ref[...])
        out_ref[j * points : (j + 1) * points, :] = total.astype(BF16)


VMEM = pl.BlockSpec(memory_space=pltpu.VMEM)
SMEM = pl.BlockSpec(memory_space=pltpu.SMEM)
ANY = pl.BlockSpec(memory_space=pl.ANY)


def per_device(
    n_dev,
    n_group,
    features,
    coords,
    near_pairs,
    parent_two,
    parent_three,
    rates,
    w_near,
    restrict,
    w_two,
    w_three,
    w_four,
    coupling,
    expand,
    w_out,
):
    points_n, channels = features.shape
    points, s_rows = expand.shape
    blocks = points_n // points
    nodes = parent_three.shape[0]
    slots_n = n_dev * SLOTS
    slice_rows = s_rows // n_dev
    nodes3 = coupling.shape[0] // n_group
    rows = slice_rows * nodes
    shape = jax.ShapeDtypeStruct
    par = jnp.repeat(parent_two, ROWS)
    p3 = jnp.tile(parent_three, slice_rows)
    vals, pos_p, pos_q, send_v, send_q, pick_p, partial, index = pl.pallas_call(
        functools.partial(prepare, n_dev),
        out_shape=(
            shape((blocks, points, channels), BF16),
            shape((blocks, AUG, points), BF16),
            shape((blocks, AUG, points), BF16),
            shape((slots_n, points, channels), BF16),
            shape((slots_n, AUG, points), BF16),
            shape((slots_n, AUG, points), BF16),
            shape((s_rows, nodes, channels), BF16),
            shape((slots_n,), jnp.int32),
        ),
        in_specs=[SMEM] + [VMEM] * 5,
        out_specs=(VMEM,) * 7 + (SMEM,),
        scratch_shapes=[
            pltpu.SMEM((2 * n_dev,), jnp.int32),
            pltpu.VMEM((blocks, s_rows, channels), F32),
        ],
        name="prepare",
    )(near_pairs, features, coords, par.reshape(1, -1), w_near, restrict)
    dma = pltpu.SemaphoreType.DMA
    own, side, down = pl.pallas_call(
        functools.partial(exchange, n_dev, n_group),
        out_shape=(
            shape((blocks, points, channels), F32),
            shape((n_dev, SLOTS, points, channels), BF16),
            shape((n_dev, slice_rows, nodes, channels), BF16),
        ),
        in_specs=[SMEM] + [VMEM] * 4 + [ANY] * 3 + [VMEM] * 6,
        out_specs=(VMEM,) * 3,
        scratch_shapes=[
            pltpu.VMEM((n_dev, SLOTS, points, channels), BF16),
            pltpu.VMEM((n_dev, SLOTS, AUG, points), BF16),
            pltpu.VMEM((n_dev, slice_rows, nodes, channels), BF16),
            pltpu.VMEM((n_group, slice_rows * nodes3, channels), BF16),
            pltpu.VMEM((n_dev, slice_rows, nodes, channels), BF16),
            pltpu.VMEM((slice_rows * nodes3, channels), BF16),
            pltpu.VMEM((slice_rows, nodes, channels), BF16),
            dma((2, n_dev)),
            dma((2, n_dev)),
            dma((2, n_dev)),
            dma((2, n_group)),
            dma((2, n_dev)),
            dma((3,)),
        ],
        compiler_params=pltpu.CompilerParams(
            collective_id=0, has_side_effects=True, vmem_limit_bytes=60 * 1024 * 1024
        ),
        name="exchange",
    )(
        rates,
        vals,
        pos_p,
        pos_q,
        pick_p.reshape(n_dev, SLOTS, AUG, points),
        send_v.reshape(n_dev, SLOTS, points, channels),
        send_q.reshape(n_dev, SLOTS, AUG, points),
        partial,
        p3.reshape(1, -1),
        p3.reshape(-1, 1),
        w_two,
        w_three,
        w_four,
        coupling,
    )
    return pl.pallas_call(
        functools.partial(finish, slots_n),
        out_shape=shape((points_n, channels), BF16),
        in_specs=[SMEM] + [VMEM] * 6,
        out_specs=VMEM,
        scratch_shapes=[
            pltpu.VMEM((blocks, points, channels), F32),
            pltpu.VMEM((blocks, s_rows, channels), F32),
        ],
        name="finish",
    )(
        index,
        own,
        side.reshape(slots_n, points, channels),
        down.reshape(s_rows, nodes, channels),
        par.reshape(-1, 1),
        expand,
        w_out,
    )


def solution(mesh):
    placed = (
        P(("group", "dev"), None),
        P(None, ("group", "dev")),
        P(None, "group"),
        P(("group", "dev")),
        P("group"),
    ) + (P(),) * 9
    return jax.shard_map(
        functools.partial(per_device, mesh.shape["dev"], mesh.shape["group"]),
        mesh=mesh,
        in_specs=placed,
        out_specs=P(("group", "dev"), None),
        check_vma=False,
    )
```

```python
import functools
import math

import jax
import jax.numpy as jnp
from jax import lax
from jax.experimental import pallas as pl
from jax.experimental.pallas import tpu as pltpu
from jax.sharding import PartitionSpec as P

CAP = 2
SLOTS = 2 * CAP
AUG = 16
ROWS = 8
LOG2E = math.log2(math.e)
MESH = pl.DeviceIdType.MESH
F32 = jnp.float32
BF16 = jnp.bfloat16


def mm(a, b):
    return jnp.dot(a, b, preferred_element_type=F32)


def iota(shape, axis):
    return lax.broadcasted_iota(jnp.int32, shape, axis)


def prepare(
    n_dev,
    pairs_ref,
    feat_ref,
    coords_ref,
    par_ref,
    wnear_ref,
    restrict_ref,
    vals_ref,
    pos_p_ref,
    pos_q_ref,
    send_v_ref,
    send_q_ref,
    pick_p_ref,
    partial_ref,
    index_ref,
    count_ref,
    level_ref,
):
    me = lax.axis_index("dev")
    blocks, points, channels = vals_ref.shape
    pairs_n = pairs_ref.shape[1]
    s_rows, nodes, _ = partial_ref.shape

    def clear(i, _):
        index_ref[i] = -1
        return 0

    lax.fori_loop(0, n_dev * SLOTS, clear, 0)

    def clear_count(i, _):
        count_ref[i] = 0
        return 0

    lax.fori_loop(0, n_dev * 2, clear_count, 0)

    def one_pair(k, _):
        a = pairs_ref[0, k]
        b = pairs_ref[1, k]
        own_a = a // blocks
        own_b = b // blocks

        @pl.when(own_a == me)
        def _():
            rank = count_ref[own_b]
            index_ref[own_b * SLOTS + rank] = a % blocks
            count_ref[own_b] = rank + 1

        @pl.when(own_b == me)
        def _():
            rank = count_ref[n_dev + own_a]
            index_ref[own_a * SLOTS + CAP + rank] = b % blocks
            count_ref[n_dev + own_a] = rank + 1

        return 0

    lax.fori_loop(0, pairs_n, one_pair, 0)

    xyz = coords_ref[...].astype(F32)
    norm = jnp.sum(xyz * xyz, axis=0, keepdims=True)
    one = norm.astype(BF16).astype(F32)
    two = (norm - one).astype(BF16).astype(F32)
    three = norm - one - two
    ones = jnp.ones_like(norm)
    pad = jnp.zeros((AUG - 9, norm.shape[1]), F32)
    aug_p = jnp.concatenate([-2.0 * xyz, one, two, three, ones, ones, ones, pad], axis=0).astype(BF16)
    aug_q = jnp.concatenate([xyz, ones, ones, ones, one, two, three, pad], axis=0).astype(BF16)
    for j in range(blocks):
        pos_p_ref[j] = aug_p[:, j * points : (j + 1) * points]
        pos_q_ref[j] = aug_q[:, j * points : (j + 1) * points]
        block = feat_ref[pl.ds(j * points, points), :]
        vals_ref[j] = mm(block, wnear_ref[...]).astype(BF16)
        level_ref[j] = mm(restrict_ref[...], block).astype(BF16).astype(F32)

    rows, cols = ROWS * nodes, blocks * ROWS
    row, col = iota((rows, cols), 0), iota((rows, cols), 1)
    spread = ((row // nodes == col % ROWS) & (row % nodes == par_ref[...])).astype(F32).astype(BF16)
    for c in range(s_rows // ROWS):
        part = level_ref[:, c * ROWS : (c + 1) * ROWS, :].reshape(cols, channels).astype(BF16)
        partial_ref[c * ROWS : (c + 1) * ROWS] = (
            mm(spread, part).astype(BF16).reshape(ROWS, nodes, channels)
        )

    def pick(i, _):
        local = jnp.maximum(index_ref[i], 0)
        to = (i // SLOTS) * SLOTS + (i + CAP) % SLOTS
        send_v_ref[to] = vals_ref[local]
        send_q_ref[to] = pos_q_ref[local]
        pick_p_ref[i] = pos_p_ref[local]
        return 0

    lax.fori_loop(0, n_dev * SLOTS, pick, 0)


def table_apply(pos_p, pos_q, values, rates_ref, heads):
    d2 = lax.dot_general(pos_p, pos_q, (((0,), (0,)), ((), ())), preferred_element_type=F32)
    channels = values.shape[1]
    head_of = iota(values.shape, 1) // (channels // heads)
    total = None
    for h in range(heads):
        kernel = jnp.exp2((d2 * (rates_ref[h] * (-LOG2E))).astype(BF16))
        term = mm(kernel, jnp.where(head_of == h, values, jnp.zeros_like(values)))
        total = term if total is None else total + term
    return total


def exchange(
    n_dev,
    n_group,
    rates_ref,
    vals_ref,
    pos_p_ref,
    pos_q_ref,
    pick_p_ref,
    send_v_ref,
    send_q_ref,
    partial_ref,
    p3_lane_ref,
    p3_col_ref,
    wtwo_ref,
    wthree_ref,
    wfour_ref,
    coupling_ref,
    self_ref,
    side_ref,
    down_ref,
    got_v,
    got_q,
    got_part,
    sum_part,
    got_three,
    got_down,
    three_buf,
    v_sems,
    q_sems,
    part_sems,
    three_sems,
    down_sems,
    local_sems,
):
    me = lax.axis_index("dev")
    mine = lax.axis_index("group")
    heads = rates_ref.shape[0]
    blocks = vals_ref.shape[0]
    s_rows, nodes, channels = partial_ref.shape
    slice_rows = s_rows // n_dev
    nodes3 = coupling_ref.shape[0] // n_group
    half_n = n_dev // 2
    stages = n_dev.bit_length() - 1
    bits = [(me // (1 << t)) % 2 for t in range(stages)]

    def peer_of(mask):
        other = 0
        for t in range(stages):
            flip = (mask // (1 << t)) % 2
            other = other + (bits[t] + flip - 2 * bits[t] * flip) * (1 << t)
        return other

    barrier = pltpu.get_barrier_semaphore()

    def greet(k, _):
        pl.semaphore_signal(barrier, inc=1, device_id={"dev": peer_of(k)}, device_id_type=MESH)
        return 0

    def greet_group(k, _):
        pl.semaphore_signal(barrier, inc=1, device_id={"group": (mine + k) % n_group}, device_id_type=MESH)
        return 0

    lax.fori_loop(1, n_dev, greet, 0)
    lax.fori_loop(1, n_group, greet_group, 0)

    def own_copies():
        return (
            pltpu.make_async_copy(send_v_ref.at[me], got_v.at[me], local_sems.at[0]),
            pltpu.make_async_copy(send_q_ref.at[me], got_q.at[me], local_sems.at[1]),
        )

    for copy in own_copies():
        copy.start()
    pl.semaphore_wait(barrier, n_dev - 1 + n_group - 1)

    def dev_copy(src, dst, sems, k, mask):
        return pltpu.make_async_remote_copy(
            src_ref=src,
            dst_ref=dst,
            send_sem=sems.at[0, k],
            recv_sem=sems.at[1, k],
            device_id={"dev": peer_of(mask)},
            device_id_type=MESH,
        )

    upper = me // half_n
    wide_rows = 2 * slice_rows
    mine_rows = pl.ds((me % half_n) * wide_rows + upper * slice_rows, slice_rows)

    def near_copy(mask):
        src = partial_ref.at[pl.ds((peer_of(mask) % half_n) * wide_rows, wide_rows)]
        return dev_copy(src, got_part.at[mask], part_sems, mask, mask)

    def across_copy():
        return dev_copy(sum_part.at[0], sum_part.at[1], part_sems, half_n, half_n)

    def near_sum(side):
        own = partial_ref[pl.ds((me % half_n) * wide_rows + side * slice_rows, slice_rows)].astype(F32)
        for mask in range(1, half_n):
            own = own + got_part[mask, pl.ds(side * slice_rows, slice_rows)].astype(F32)
        return own

    def down_across():
        held = got_down.at[mine_rows]
        return dev_copy(held, held, down_sems, half_n, half_n)

    def down_near(mask):
        held = got_down.at[pl.ds((me % half_n) * wide_rows, wide_rows)]
        return dev_copy(held, held, down_sems, mask, mask)

    def v_copy(mask, slot):
        return dev_copy(
            send_v_ref.at[peer_of(mask), slot], got_v.at[me, slot], v_sems, slot * n_dev + mask, mask
        )

    def q_copy(mask):
        return dev_copy(send_q_ref.at[peer_of(mask)], got_q.at[me], q_sems, mask, mask)

    def three_copy(k):
        return pltpu.make_async_remote_copy(
            src_ref=three_buf,
            dst_ref=got_three.at[mine],
            send_sem=three_sems.at[0, k],
            recv_sem=three_sems.at[1, k],
            device_id={"group": (mine + k) % n_group},
            device_id_type=MESH,
        )

    def each(fn, low, high):
        def body(k, _):
            fn(k)
            return 0

        lax.fori_loop(low, high, body, 0)

    def feed(slot):
        each(lambda k: v_copy(k, slot).start(), half_n, n_dev)
        each(lambda k: v_copy(k, slot).start(), 1, half_n)

    done = [0]

    def self_tables(count):
        low, high = done[0], min(done[0] + count, blocks)
        done[0] = high

        def body(j, _):
            self_ref[j] = table_apply(pos_p_ref[j], pos_q_ref[j], vals_ref[j], rates_ref, heads)
            return 0

        if high > low:
            lax.fori_loop(low, high, body, 0)

    each(lambda k: near_copy(k).start(), 1, half_n)
    each(lambda k: q_copy(k).start(), 1, n_dev)
    feed(0)
    self_tables(4)
    each(lambda k: near_copy(k).wait(), 1, half_n)
    sum_part[0] = near_sum(1 - upper).astype(BF16)
    self_tables(1)
    across_copy().start()
    feed(1)
    own_sum = near_sum(upper)
    self_tables(5)
    across_copy().wait()

    rows = slice_rows * nodes
    rows3 = slice_rows * nodes3
    flat = (own_sum + sum_part[1].astype(F32)).reshape(rows, channels).astype(BF16)
    two = jax.nn.gelu(mm(flat, wtwo_ref[...])).astype(BF16)
    row, col = iota((rows3, rows), 0), iota((rows3, rows), 1)
    select = ((row // nodes3 == col // nodes) & (row % nodes3 == p3_lane_ref[...])).astype(F32).astype(BF16)
    three_buf[...] = (mm(select, two) * (nodes3 / nodes)).astype(BF16)
    lifted = mm(two, wfour_ref[...])
    self_tables(1)
    each(lambda k: three_copy(k).start(), 1, n_group)
    got_three[mine] = three_buf[...]
    self_tables(1)

    all3 = coupling_ref.shape[0]
    row, col = iota((rows3, all3), 0), iota((rows3, all3), 1)
    left = mm((col == mine * nodes3 + row % nodes3).astype(F32).astype(BF16), coupling_ref[...]).astype(BF16)
    row, col = iota((all3, n_group * rows3), 0), iota((all3, n_group * rows3), 1)
    right = (row == (col // rows3) * nodes3 + col % nodes3).astype(F32).astype(BF16)
    row, col = iota((rows3, n_group * rows3), 0), iota((rows3, n_group * rows3), 1)
    wide = jnp.where(row // nodes3 == (col % rows3) // nodes3, mm(left, right), 0.0).astype(BF16)
    row, col = iota((rows, rows3), 0), iota((rows, rows3), 1)
    lift = ((row // nodes == col // nodes3) & (p3_col_ref[...] == col % nodes3)).astype(F32).astype(BF16)

    each(lambda k: three_copy(k).wait(), 1, n_group)
    mixed = mm(wide, got_three[...].reshape(n_group * rows3, channels)).astype(BF16)
    down3 = jax.nn.gelu(mm(mixed, wthree_ref[...])).astype(BF16)
    down2 = jax.nn.gelu(lifted + mm(lift, down3)).astype(BF16).reshape(slice_rows, nodes, channels)
    got_down[mine_rows] = down2
    self_tables(1)
    down_across().start()
    feed(2)
    self_tables(blocks)
    down_across().wait()
    each(lambda k: down_near(k).start(), 1, half_n)
    feed(3)
    for copy in own_copies():
        copy.wait()
    each(lambda k: q_copy(k).wait(), 1, n_dev)

    def side_table(mask, slot):
        source = peer_of(mask)
        side_ref[source, slot] = table_apply(
            pick_p_ref[source, slot], got_q[source, slot], got_v[source, slot], rates_ref, heads
        ).astype(BF16)

    each(lambda j: side_table(0, j), 0, SLOTS)

    def arrived(slot):
        def body(k):
            v_copy(k, slot).wait()
            side_table(k, slot)

        return body

    for slot in range(SLOTS):
        each(arrived(slot), half_n, n_dev)
        each(arrived(slot), 1, half_n)
    each(lambda k: down_near(k).wait(), 1, half_n)
    down_ref[...] = got_down[...]


def finish(slots_n, index_ref, self_ref, side_ref, down_ref, par_ref, expand_ref, wout_ref, out_ref, acc, parent_down):
    blocks, points, channels = self_ref.shape
    s_rows, nodes, _ = down_ref.shape
    rows, cols = blocks * ROWS, ROWS * nodes
    row, col = iota((rows, cols), 0), iota((rows, cols), 1)
    gather = ((row % ROWS == col // nodes) & (par_ref[...] == col % nodes)).astype(F32).astype(BF16)
    for c in range(s_rows // ROWS):
        part = down_ref[c * ROWS : (c + 1) * ROWS].reshape(cols, channels)
        parent_down[:, c * ROWS : (c + 1) * ROWS, :] = mm(gather, part).reshape(blocks, ROWS, channels)
    acc[...] = self_ref[...]

    def add(i, _):
        local = index_ref[i]

        @pl.when(local >= 0)
        def _():
            acc[local] += side_ref[i].astype(F32)

        return 0

    lax.fori_loop(0, slots_n, add, 0)
    for j in range(blocks):
        far = mm(expand_ref[...], parent_down[j].astype(BF16)).astype(BF16)
        total = acc[j] * (points ** (-0.5)) + mm(far, wout_ref[...])
        out_ref[j * points : (j + 1) * points, :] = total.astype(BF16)


VMEM = pl.BlockSpec(memory_space=pltpu.VMEM)
SMEM = pl.BlockSpec(memory_space=pltpu.SMEM)
ANY = pl.BlockSpec(memory_space=pl.ANY)


def per_device(
    n_dev,
    n_group,
    features,
    coords,
    near_pairs,
    parent_two,
    parent_three,
    rates,
    w_near,
    restrict,
    w_two,
    w_three,
    w_four,
    coupling,
    expand,
    w_out,
):
    points_n, channels = features.shape
    points, s_rows = expand.shape
    blocks = points_n // points
    nodes = parent_three.shape[0]
    slots_n = n_dev * SLOTS
    slice_rows = s_rows // n_dev
    nodes3 = coupling.shape[0] // n_group
    shape = jax.ShapeDtypeStruct
    par = jnp.repeat(parent_two, ROWS)
    p3 = jnp.tile(parent_three, slice_rows)
    vals, pos_p, pos_q, send_v, send_q, pick_p, partial, index = pl.pallas_call(
        functools.partial(prepare, n_dev),
        out_shape=(
            shape((blocks, points, channels), BF16),
            shape((blocks, AUG, points), BF16),
            shape((blocks, AUG, points), BF16),
            shape((slots_n, points, channels), BF16),
            shape((slots_n, AUG, points), BF16),
            shape((slots_n, AUG, points), BF16),
            shape((s_rows, nodes, channels), BF16),
            shape((slots_n,), jnp.int32),
        ),
        in_specs=[SMEM] + [VMEM] * 5,
        out_specs=(VMEM,) * 7 + (SMEM,),
        scratch_shapes=[
            pltpu.SMEM((2 * n_dev,), jnp.int32),
            pltpu.VMEM((blocks, s_rows, channels), F32),
        ],
        name="prepare",
    )(near_pairs, features, coords, par.reshape(1, -1), w_near, restrict)
    dma = pltpu.SemaphoreType.DMA
    own, side, down = pl.pallas_call(
        functools.partial(exchange, n_dev, n_group),
        out_shape=(
            shape((blocks, points, channels), F32),
            shape((n_dev, SLOTS, points, channels), BF16),
            shape((s_rows, nodes, channels), BF16),
        ),
        in_specs=[SMEM] + [VMEM] * 4 + [ANY] * 2 + [VMEM] * 7,
        out_specs=(VMEM,) * 3,
        scratch_shapes=[
            pltpu.VMEM((n_dev, SLOTS, points, channels), BF16),
            pltpu.VMEM((n_dev, SLOTS, AUG, points), BF16),
            pltpu.VMEM((n_dev // 2, 2 * slice_rows, nodes, channels), BF16),
            pltpu.VMEM((2, slice_rows, nodes, channels), BF16),
            pltpu.VMEM((n_group, slice_rows * nodes3, channels), BF16),
            pltpu.VMEM((s_rows, nodes, channels), BF16),
            pltpu.VMEM((slice_rows * nodes3, channels), BF16),
            dma((2, SLOTS * n_dev)),
            dma((2, n_dev)),
            dma((2, n_dev)),
            dma((2, n_group)),
            dma((2, n_dev)),
            dma((2,)),
        ],
        compiler_params=pltpu.CompilerParams(
            collective_id=0, has_side_effects=True, vmem_limit_bytes=60 * 1024 * 1024
        ),
        name="exchange",
    )(
        rates,
        vals,
        pos_p,
        pos_q,
        pick_p.reshape(n_dev, SLOTS, AUG, points),
        send_v.reshape(n_dev, SLOTS, points, channels),
        send_q.reshape(n_dev, SLOTS, AUG, points),
        partial,
        p3.reshape(1, -1),
        p3.reshape(-1, 1),
        w_two,
        w_three,
        w_four,
        coupling,
    )
    return pl.pallas_call(
        functools.partial(finish, slots_n),
        out_shape=shape((points_n, channels), BF16),
        in_specs=[SMEM] + [VMEM] * 6,
        out_specs=VMEM,
        scratch_shapes=[
            pltpu.VMEM((blocks, points, channels), F32),
            pltpu.VMEM((blocks, s_rows, channels), F32),
        ],
        name="finish",
    )(
        index,
        own,
        side.reshape(slots_n, points, channels),
        down,
        par.reshape(-1, 1),
        expand,
        w_out,
    )


def solution(mesh):
    placed = (
        P(("group", "dev"), None),
        P(None, ("group", "dev")),
        P(None, "group"),
        P(("group", "dev")),
        P("group"),
    ) + (P(),) * 9
    return jax.shard_map(
        functools.partial(per_device, mesh.shape["dev"], mesh.shape["group"]),
        mesh=mesh,
        in_specs=placed,
        out_specs=P(("group", "dev"), None),
        check_vma=False,
    )
```
